32 devices in a mesh: leaf: 8 (over z, x), rhs: 4 (over y, core).
Axes of the slice: x: 2, y: 2, z: 4, core: 2. Of those that a mesh axis runs over, the one named last changes fastest.
Arguments:
- charges: float32 [6144, 4096], P('leaf', 'rhs'), parts along dimension 1, may hold values from -6 to 6
- near_blocks: float32 [8, 3, 768, 768], P('leaf'), may hold values from -0.125 to 0.125
- neighbours: int32 [8, 2], P('leaf'), may hold values from 0 to 7, as said below
- compress: float32 [8, 768, 192], P('leaf'), may hold values from -0.21875 to 0.21875
- transfer: float32 [8, 3, 2, 192, 192], P('leaf'), may hold values from -0.3125 to 0.3125
- expand: float32 [8, 768, 192], P('leaf'), may hold values from -0.4375 to 0.4375
Outputs:
- potential: float32 [6144, 4096], P('leaf', 'rhs'), parts along dimension 1
The draws below stay inside these ranges and needn't reach their ends.
There are 4 independent parts, one for each index of `rhs`. The reference program is written for one: setup_inputs(seed, part) draws one part's arguments, and reference() takes and returns one part's arrays. A program takes and returns all parts, laid end to end along the dimension named above; an argument that names none is the same for every part. Nothing has to cross between parts.
Inputs may be any that keep to these rules, and one draw needn't show every extreme that they name: `neighbours`: row i lists two different leaves, each of (i - 2), (i - 1), (i + 1), (i + 2) modulo 8; never i itself.
All inputs are finite; a program needn't handle non-finite values.
Results may differ from the reference program's by a relative error of at most 0.0001.
Values sent between devices are 32-bit elements; how exact they have to be, the bound alone decides.
No kernel may reach another device: no remote copies, remote signals or barrier semaphores. Data moves between devices by JAX's collectives and lax.ppermute only.
A program may use at most 128 MiB of HBM per device.

```python
import jax
import jax.numpy as jnp
from jax import lax

LEAF_ROWS = 768
RANK = 192
COLS = 1024
LEAVES = 8
LEVELS = 3
ROWS = 6144


def draw_neighbours(key, part):
    key_one = jax.random.fold_in(key, 11)
    key_two = jax.random.fold_in(key, 23)
    first = jax.random.randint(key_one, (LEAVES,), 0, 4)
    second = (first + jax.random.randint(key_two, (LEAVES,), 1, 4)) % 4
    picks = jnp.stack([first, second], axis=1)
    offsets = jnp.where(picks < 2, picks - 2, picks - 1)
    leaf_ids = jnp.arange(LEAVES, dtype=jnp.int32)[:, None]
    return ((leaf_ids + offsets) % LEAVES).astype(jnp.int32)


def block_levels(key, extent, split, smallest, largest):
    def one(axis_at, shards_of):
        draws = jax.random.uniform(jax.random.fold_in(jax.random.fold_in(key, 6), axis_at), (shards_of,), jnp.float32, smallest / len(split), largest / len(split))
        return jnp.repeat(jnp.exp(draws), extent[axis_at] // shards_of).reshape((-1,) + (1,) * (len(extent) - axis_at - 1))

    loudness = one(*split[0])
    for cut in split[1:]:
        loudness = loudness * one(*cut)
    return loudness


def bell_draw(stream_key, extent, spread, bound, shards=(), kind=jnp.bfloat16):
    array = jax.random.normal(stream_key, extent, jnp.float32) * spread
    if len(shards) > 0:
        array = block_levels(stream_key, extent, shards, -0.22, 0.18) * array
    return jnp.clip(array, min=-bound, max=bound).astype(kind)


def setup_inputs(seed: int = 0, part: int = 0) -> dict:
    seeds = jax.random.split(jax.random.key(seed), 7)
    part_keys = jax.random.split(jax.random.fold_in(seeds[6], part), 7)
    return {
        "charges": bell_draw(part_keys[0], (ROWS, COLS), 1.0, 6.0, ((0, 8),), jnp.float32),
        "near_blocks": bell_draw(seeds[1], (LEAVES, 3, LEAF_ROWS, LEAF_ROWS), (3 * LEAF_ROWS) ** -0.5, 0.125, ((0, 8),), jnp.float32),
        "neighbours": draw_neighbours(jax.random.fold_in(seeds[6], 71), part),
        "compress": bell_draw(seeds[3], (LEAVES, LEAF_ROWS, RANK), LEAF_ROWS ** -0.5, 0.21875, ((0, 8),), jnp.float32),
        "transfer": bell_draw(seeds[4], (LEAVES, LEVELS, 2, RANK, RANK), (2 * RANK) ** -0.5, 0.3125, ((0, 8),), jnp.float32),
        "expand": bell_draw(seeds[5], (LEAVES, LEAF_ROWS, RANK), RANK ** -0.5, 0.4375, ((0, 8),), jnp.float32),
    }


def reference(charges, near_blocks, neighbours, compress, transfer, expand):
    hi = lax.Precision.HIGHEST
    blocks = charges.reshape(LEAVES, LEAF_ROWS, COLS)
    first = blocks[neighbours[:, 0]]
    second = blocks[neighbours[:, 1]]
    near = jnp.einsum('lab,lbc->lac', near_blocks[:, 0], blocks, precision=hi)
    near = near + jnp.einsum('lab,lbc->lac', near_blocks[:, 1], first, precision=hi)
    near = near + jnp.einsum('lab,lbc->lac', near_blocks[:, 2], second, precision=hi)
    coeffs = jnp.einsum('lar,lac->lrc', compress, blocks, precision=hi)
    leaf_ids = jnp.arange(LEAVES, dtype=jnp.int32)
    for level in range(LEVELS):
        partner_ids = jnp.bitwise_xor(leaf_ids, jnp.int32(1 << level))
        partner_coeffs = coeffs[partner_ids]
        coeffs = jnp.einsum('lrs,lsc->lrc', transfer[:, level, 0], coeffs, precision=hi) + jnp.einsum('lrs,lsc->lrc', transfer[:, level, 1], partner_coeffs, precision=hi)
    far = jnp.einsum('lar,lrc->lac', expand, coeffs, precision=hi)
    return (near + far).reshape(LEAVES * LEAF_ROWS, COLS)
```

```python
import jax
import jax.numpy as jnp
from jax import lax
from jax.sharding import PartitionSpec as P


HIGH = lax.Precision.HIGH


def dot(a, b):
    return jnp.dot(a, b, precision=HIGH)


def partner(value, distance):
    return lax.ppermute(value, "leaf", [(i, i ^ 1 << distance) for i in range(lax.axis_size("leaf"))])


def two_along(value, sense):
    count = lax.axis_size("leaf")
    pairs = [(i, (i + (2 if i % 2 else -2) * sense) % count) for i in range(count)]
    return lax.ppermute(value, "leaf", pairs)


def per_device(charges, near_blocks, neighbours, compress, transfer, expand):
    count = lax.axis_size("leaf")
    here = lax.axis_index("leaf")
    side = jnp.where(here % 2 == 0, 1, -1)
    levels = count.bit_length() - 1
    last = levels - 1

    offsets = (neighbours[0] - here) % count
    offsets = jnp.where(offsets > count // 2, offsets - count, offsets)

    def weight(step):
        second = jnp.where(offsets[1] == step, near_blocks[0, 2], 0.0)
        return jnp.where(offsets[0] == step, near_blocks[0, 1], second)

    def add(total, a, b):
        return lax.optimization_barrier(total + dot(a, b))

    far_side = two_along(charges, 1)
    near_side = two_along(charges, -1)
    mate = partner(charges, 0)
    relay = partner(far_side, 0)
    coeffs = jnp.einsum("ar,ac->rc", compress[0], charges, precision=HIGH)
    for level in range(levels):
        other = partner(coeffs, level)
        if level < last:
            coeffs = dot(transfer[0, level, 0], coeffs) + dot(transfer[0, level, 1], other)
    far_own = dot(expand[0], transfer[0, last, 0])
    far_other = dot(expand[0], transfer[0, last, 1])

    total = lax.optimization_barrier(dot(near_blocks[0, 0], charges))
    total = add(total, weight(2 * side), far_side)
    total = add(total, weight(side), mate)
    total = add(total, far_own, coeffs)
    total = add(total, weight(-side), relay)
    total = add(total, weight(-2 * side), near_side)
    total = add(total, far_other, other)
    return total


def solution(mesh):
    in_specs = (
        P("leaf", "rhs"),
        P("leaf", None, None, None),
        P("leaf", None),
        P("leaf", None, None),
        P("leaf", None, None, None, None),
        P("leaf", None, None),
    )
    out_specs = P("leaf", "rhs")
    return jax.shard_map(
        per_device, mesh=mesh, in_specs=in_specs, out_specs=out_specs, check_vma=False
    )
```

```python
import jax
import jax.numpy as jnp
from jax import lax
from jax.experimental import pallas as pl
from jax.experimental.pallas import tpu as pltpu
from jax.sharding import PartitionSpec as P


HIGH = lax.Precision.HIGH


def dot(a, b):
    return jnp.dot(a, b, precision=HIGH)


def partner(value, distance, senders=None):
    everyone = range(lax.axis_size("leaf"))
    return lax.ppermute(value, "leaf", [(i, i ^ 1 << distance) for i in senders or everyone])


def two_along(sense, count):
    return [(i, (i + (2 if i % 2 else -2) * sense) % count) for i in range(count)]


def eighths(rows, *counts):
    edges = [rows * count // 64 * 8 for count in counts] + [rows]
    return list(zip([0] + edges, edges))


def halves(value):
    high = value.astype(jnp.bfloat16)
    return high, (value - high.astype(jnp.float32)).astype(jnp.bfloat16)


def last_terms(total_ref, w_ref, near_ref, far_ref, first_ref, second_ref, out_ref):
    result = total_ref[...]
    pairs = ((w_ref[...], near_ref[...]), (far_ref[...], first_ref[...] + second_ref[...]))
    for a, b in pairs:
        a_high, a_low = halves(a)
        b_high, b_low = halves(b)
        for left, right in ((a_high, b_low), (a_low, b_high), (a_high, b_high)):
            result = result + jnp.dot(left, right, preferred_element_type=jnp.float32)
    out_ref[...] = result


def finish(total, w, near, far, first, second):
    rows, cols = total.shape
    tile = min(cols, 256)
    strip = lambda depth: pl.BlockSpec((depth, tile), lambda j: (0, j))
    whole = lambda array: pl.BlockSpec(array.shape, lambda j: (0, 0))
    depth = w.shape[1] + far.shape[1]
    return pl.pallas_call(
        last_terms,
        grid=(cols // tile,),
        out_shape=jax.ShapeDtypeStruct(total.shape, total.dtype),
        in_specs=[
            strip(rows),
            whole(w),
            strip(near.shape[0]),
            whole(far),
            strip(first.shape[0]),
            strip(second.shape[0]),
        ],
        out_specs=strip(rows),
        cost_estimate=pl.CostEstimate(
            flops=6 * rows * cols * depth, bytes_accessed=8 * rows * cols, transcendentals=0
        ),
        compiler_params=pltpu.CompilerParams(vmem_limit_bytes=24 << 20),
    )(total, w, near, far, first, second)


def per_device(charges, near_blocks, neighbours, compress, transfer, expand):
    count = lax.axis_size("leaf")
    here = lax.axis_index("leaf")
    side = jnp.where(here % 2 == 0, 1, -1)
    levels = count.bit_length() - 1
    last = levels - 1
    middle = count // 2
    outer = [i for i in range(count) if not middle // 2 <= i < count - middle // 2]
    inner = [i for i in range(count) if middle // 2 <= i < count - middle // 2]
    is_inner = (here >= middle // 2) & (here < count - middle // 2)
    shift = two_along(-1, count)
    central = [(s, t) for s, t in shift if abs(s - t) == 2 and (s < middle) != (t < middle)]
    others = [pair for pair in shift if pair not in central]
    over_middle = (here == middle) | (here == middle - 1)
    far_cuts = eighths(charges.shape[0], 4)
    near_cuts = eighths(charges.shape[0], 2, 6)

    offsets = (neighbours[0] - here) % count
    offsets = jnp.where(offsets > count // 2, offsets - count, offsets)

    def weight(step):
        second = jnp.where(offsets[1] == step, near_blocks[0, 2], 0.0)
        return jnp.where(offsets[0] == step, near_blocks[0, 1], second)

    def move(value, pairs):
        return lax.ppermute(value, "leaf", pairs)

    def add(total, a, b):
        return lax.optimization_barrier(total + dot(a, b))

    far, near, relay = [], [], []
    coeffs = jnp.einsum("ar,ac->rc", compress[0], charges, precision=HIGH)
    later, coeffs = lax.optimization_barrier((charges, coeffs))
    for part, (low, high) in enumerate(far_cuts):
        far.append(move((later if part else charges)[low:high], two_along(1, count)))
        relay.append(partner(far[part], 0))
    low, high = near_cuts[0]
    near_central = move(later[low:high], central)
    near_others = move(later[low:high], others)
    near.append(jnp.where(over_middle, near_central, near_others))
    for part, (low, high) in enumerate(near_cuts[1:], 1):
        near.append(move(later[low:high], shift))
    mate = partner(charges, 0)
    for level in range(last):
        other = partner(coeffs, level)
        coeffs = dot(transfer[0, level, 0], coeffs) + dot(transfer[0, level, 1], other)
    from_outer = partner(coeffs, last, outer)
    from_inner = partner(coeffs, last, inner)
    ends = jnp.concatenate([transfer[0, last, 0], transfer[0, last, 1]], axis=1)
    far_own, far_other = jnp.split(dot(expand[0], ends), 2, axis=1)

    w_far, w_near, w_mate, w_relay = (weight(s) for s in (2 * side, -2 * side, side, -side))

    def add_near(total, part):
        low, high = near_cuts[part]
        return add(total, w_near[:, low:high], near[part])

    total = lax.optimization_barrier(dot(near_blocks[0, 0], charges))
    total = add(total, far_own, coeffs)
    total = add(total, w_mate, mate)
    total = add(total, w_far, jnp.concatenate(far))
    total = add_near(total, 0)
    total = add_near(total, 1)
    total = add(total, w_relay, jnp.concatenate(relay))
    low, high = near_cuts[2]
    return finish(total, w_near[:, low:high], near[2], far_other, from_outer, from_inner)


def solution(mesh):
    in_specs = (
        P("leaf", "rhs"),
        P("leaf", None, None, None),
        P("leaf", None),
        P("leaf", None, None),
        P("leaf", None, None, None, None),
        P("leaf", None, None),
    )
    out_specs = P("leaf", "rhs")
    return jax.shard_map(
        per_device, mesh=mesh, in_specs=in_specs, out_specs=out_specs, check_vma=False
    )
```

```python
import jax
import jax.numpy as jnp
from jax import lax
from jax.experimental import pallas as pl
from jax.experimental.pallas import tpu as pltpu
from jax.sharding import PartitionSpec as P


HIGH = lax.Precision.HIGH


def dot(a, b):
    return jnp.dot(a, b, precision=HIGH)


def partner(value, distance, senders=None):
    everyone = range(lax.axis_size("leaf"))
    return lax.ppermute(value, "leaf", [(i, i ^ 1 << distance) for i in senders or everyone])


def two_along(sense, count):
    return [(i, (i + (2 if i % 2 else -2) * sense) % count) for i in range(count)]


def eighths(rows, *counts):
    edges = [rows * count // 64 * 8 for count in counts] + [rows]
    return list(zip([0] + edges, edges))


def three_pass(weight):
    high = lax.reduce_precision(weight, exponent_bits=8, mantissa_bits=7)
    parts = [high, weight - high, high]
    return jnp.concatenate([part.astype(jnp.bfloat16) for part in parts], axis=1)


def last_term(total_ref, left_ref, right_ref, out_ref, strips, sems):
    tile = strips.shape[2]
    copies = []
    for part in range(strips.shape[0]):
        columns = pl.ds(part * tile, tile)
        value = right_ref[:, columns]
        high = value.astype(jnp.bfloat16)
        low = (value - high.astype(jnp.float32)).astype(jnp.bfloat16)
        right = jnp.concatenate([high, high, low])
        term = jnp.dot(left_ref[...], right, preferred_element_type=jnp.float32)
        strips[part] = total_ref[:, columns] + term
        copy = pltpu.make_async_copy(strips.at[part], out_ref.at[:, columns], sems.at[part])
        copy.start()
        copies.append(copy)
    for copy in copies:
        copy.wait()


def finish(total, left, right):
    rows, cols = total.shape
    tile = min(cols, 256)
    local = pltpu.VMEM
    operands = [pltpu.with_memory_space_constraint(value, local) for value in (total, left, right)]
    depth = left.shape[1]
    return pl.pallas_call(
        last_term,
        out_shape=jax.ShapeDtypeStruct(total.shape, total.dtype),
        in_specs=[pl.BlockSpec(memory_space=local)] * len(operands),
        out_specs=pl.BlockSpec(memory_space=pl.ANY),
        scratch_shapes=[
            pltpu.VMEM((cols // tile, rows, tile), total.dtype),
            pltpu.SemaphoreType.DMA((cols // tile,)),
        ],
        cost_estimate=pl.CostEstimate(
            flops=2 * rows * cols * depth, bytes_accessed=8 * rows * cols, transcendentals=0
        ),
        compiler_params=pltpu.CompilerParams(vmem_limit_bytes=24 << 20),
    )(*operands)


def per_device(charges, near_blocks, neighbours, compress, transfer, expand):
    count = lax.axis_size("leaf")
    here = lax.axis_index("leaf")
    side = jnp.where(here % 2 == 0, 1, -1)
    levels = count.bit_length() - 1
    last = levels - 1
    middle = count // 2
    outer = [i for i in range(count) if not middle // 2 <= i < count - middle // 2]
    inner = [i for i in range(count) if middle // 2 <= i < count - middle // 2]
    is_inner = (here >= middle // 2) & (here < count - middle // 2)
    shift = two_along(-1, count)
    central = [(s, t) for s, t in shift if abs(s - t) == 2 and (s < middle) != (t < middle)]
    others = [pair for pair in shift if pair not in central]
    over_middle = (here == middle) | (here == middle - 1)
    cuts = eighths(charges.shape[0], 4, 7)

    offsets = (neighbours[0] - here) % count
    offsets = jnp.where(offsets > count // 2, offsets - count, offsets)

    def weight(step):
        second = jnp.where(offsets[1] == step, near_blocks[0, 2], 0.0)
        return jnp.where(offsets[0] == step, near_blocks[0, 1], second)

    def move(value, pairs):
        return lax.ppermute(value, "leaf", pairs)

    def add(total, a, b):
        return lax.optimization_barrier(total + dot(a, b))

    far, near, relay = [], [], []
    coeffs = jnp.einsum("ar,ac->rc", compress[0], charges, precision=HIGH)
    later, coeffs = lax.optimization_barrier((charges, coeffs))
    for part, (low, high) in enumerate(cuts):
        far.append(move((later if part else charges)[low:high], two_along(1, count)))
        relay.append(partner(far[part], 0))
    low, high = cuts[0]
    near_central = move(later[low:high], central)
    near_others = move(later[low:high], others)
    near.append(jnp.where(over_middle, near_central, near_others))
    for part, (low, high) in enumerate(cuts[1:], 1):
        near.append(move(later[low:high], shift))
    mate = partner(charges, 0)
    for level in range(last):
        other = partner(coeffs, level)
        coeffs = dot(transfer[0, level, 0], coeffs) + dot(transfer[0, level, 1], other)
    from_outer = partner(coeffs, last, outer)
    from_inner = partner(coeffs, last, inner)
    ends = jnp.concatenate([transfer[0, last, 0], transfer[0, last, 1]], axis=1)
    far_own, far_other = jnp.split(dot(expand[0], ends), 2, axis=1)

    w_far, w_near, w_mate, w_relay = (weight(s) for s in (2 * side, -2 * side, side, -side))

    def add_near(total, part):
        low, high = cuts[part]
        return add(total, w_near[:, low:high], near[part])

    total = lax.optimization_barrier(dot(near_blocks[0, 0], charges))
    total = add(total, far_own, coeffs)
    total = add(total, w_mate, mate)
    total = add(total, w_far, jnp.concatenate(far))
    total = add_near(total, 0)
    low, high = cuts[-1]
    total = add(total, w_relay[:, :low], jnp.concatenate(relay[:-1]))
    total = add(total, w_relay[:, low:high], relay[-1])
    total = add_near(total, 1)
    total = add(total, far_other, jnp.where(is_inner, from_outer, from_inner))
    low, high = cuts[-1]
    return finish(total, three_pass(w_near[:, low:high]), near[-1])


def solution(mesh):
    in_specs = (
        P("leaf", "rhs"),
        P("leaf", None, None, None),
        P("leaf", None),
        P("leaf", None, None),
        P("leaf", None, None, None, None),
        P("leaf", None, None),
    )
    out_specs = P("leaf", "rhs")
    return jax.shard_map(
        per_device, mesh=mesh, in_specs=in_specs, out_specs=out_specs, check_vma=False
    )
```

```python
import jax
import jax.numpy as jnp
from jax import lax
from jax.experimental import pallas as pl
from jax.experimental.pallas import tpu as pltpu
from jax.sharding import PartitionSpec as P


HIGH = lax.Precision.HIGH


def dot(a, b):
    return jnp.dot(a, b, precision=HIGH)


def partner(value, distance, senders=None):
    everyone = range(lax.axis_size("leaf"))
    return lax.ppermute(value, "leaf", [(i, i ^ 1 << distance) for i in senders or everyone])


def two_along(sense, count):
    return [(i, (i + (2 if i % 2 else -2) * sense) % count) for i in range(count)]


def eighths(rows, *counts):
    edges = [rows * count // 64 * 8 for count in counts] + [rows]
    return list(zip([0] + edges, edges))


def three_pass(weight):
    high = lax.reduce_precision(weight, exponent_bits=8, mantissa_bits=7)
    parts = [high, weight - high, high]
    return jnp.concatenate([part.astype(jnp.bfloat16) for part in parts], axis=1)


def last_term(total_ref, left_ref, right_ref, out_ref, strips, sems):
    tile = strips.shape[2]
    copies = []
    for part in range(strips.shape[0]):
        columns = pl.ds(part * tile, tile)
        value = right_ref[:, columns]
        high = value.astype(jnp.bfloat16)
        low = (value - high.astype(jnp.float32)).astype(jnp.bfloat16)
        right = jnp.concatenate([high, high, low])
        term = jnp.dot(left_ref[...], right, preferred_element_type=jnp.float32)
        strips[part] = total_ref[:, columns] + term
        copy = pltpu.make_async_copy(strips.at[part], out_ref.at[:, columns], sems.at[part])
        copy.start()
        copies.append(copy)
    for copy in copies:
        copy.wait()


def finish(total, left, right):
    rows, cols = total.shape
    tile = min(cols, 256)
    local = pltpu.VMEM
    operands = [pltpu.with_memory_space_constraint(value, local) for value in (total, left, right)]
    depth = left.shape[1]
    return pl.pallas_call(
        last_term,
        out_shape=jax.ShapeDtypeStruct(total.shape, total.dtype),
        in_specs=[pl.BlockSpec(memory_space=local)] * len(operands),
        out_specs=pl.BlockSpec(memory_space=pl.ANY),
        scratch_shapes=[
            pltpu.VMEM((cols // tile, rows, tile), total.dtype),
            pltpu.SemaphoreType.DMA((cols // tile,)),
        ],
        cost_estimate=pl.CostEstimate(
            flops=2 * rows * cols * depth, bytes_accessed=8 * rows * cols, transcendentals=0
        ),
        compiler_params=pltpu.CompilerParams(vmem_limit_bytes=24 << 20),
    )(*operands)


def copy_rows(from_ref, to_ref, sem):
    copy = pltpu.make_async_copy(from_ref.at[pl.ds(0, to_ref.shape[0])], to_ref, sem)
    copy.start()
    copy.wait()


def first_rows(value, rows):
    shape = (rows, value.shape[1])
    return pl.pallas_call(
        copy_rows,
        out_shape=pltpu.VMEM(shape, value.dtype),
        in_specs=[pl.BlockSpec(memory_space=pl.ANY)],
        out_specs=pl.BlockSpec(memory_space=pltpu.VMEM),
        scratch_shapes=[pltpu.SemaphoreType.DMA(())],
        cost_estimate=pl.CostEstimate(
            flops=0, bytes_accessed=8 * rows * shape[1], transcendentals=0
        ),
        compiler_params=pltpu.CompilerParams(vmem_limit_bytes=8 << 20),
    )(value)


def per_device(charges, near_blocks, neighbours, compress, transfer, expand):
    count = lax.axis_size("leaf")
    here = lax.axis_index("leaf")
    side = jnp.where(here % 2 == 0, 1, -1)
    levels = count.bit_length() - 1
    last = levels - 1
    middle = count // 2
    outer = [i for i in range(count) if not middle // 2 <= i < count - middle // 2]
    inner = [i for i in range(count) if middle // 2 <= i < count - middle // 2]
    is_inner = (here >= middle // 2) & (here < count - middle // 2)
    shift = two_along(-1, count)
    central = [(s, t) for s, t in shift if abs(s - t) == 2 and (s < middle) != (t < middle)]
    others = [pair for pair in shift if pair not in central]
    over_middle = (here == middle) | (here == middle - 1)
    cuts = eighths(charges.shape[0], 4, 7)

    offsets = (neighbours[0] - here) % count
    offsets = jnp.where(offsets > count // 2, offsets - count, offsets)

    def weight(step):
        second = jnp.where(offsets[1] == step, near_blocks[0, 2], 0.0)
        return jnp.where(offsets[0] == step, near_blocks[0, 1], second)

    def move(value, pairs):
        return lax.ppermute(value, "leaf", pairs)

    def add(total, a, b):
        return lax.optimization_barrier(total + dot(a, b))

    far, near, relay = [], [], []
    coeffs = jnp.einsum("ar,ac->rc", compress[0], charges, precision=HIGH)
    later, coeffs = lax.optimization_barrier((charges, coeffs))
    for part, (low, high) in enumerate(cuts):
        rows = later[low:high] if part else first_rows(charges, high)
        far.append(move(rows, two_along(1, count)))
        relay.append(partner(far[part], 0))
    low, high = cuts[0]
    near_central = move(later[low:high], central)
    near_others = move(later[low:high], others)
    near.append(jnp.where(over_middle, near_central, near_others))
    for part, (low, high) in enumerate(cuts[1:], 1):
        near.append(move(later[low:high], shift))
    mate = partner(charges, 0)
    for level in range(last):
        other = partner(coeffs, level)
        coeffs = dot(transfer[0, level, 0], coeffs) + dot(transfer[0, level, 1], other)
    from_outer = partner(coeffs, last, outer)
    from_inner = partner(coeffs, last, inner)
    ends = jnp.concatenate([transfer[0, last, 0], transfer[0, last, 1]], axis=1)
    far_own, far_other = jnp.split(dot(expand[0], ends), 2, axis=1)

    w_far, w_near, w_mate, w_relay = (weight(s) for s in (2 * side, -2 * side, side, -side))

    def add_near(total, part):
        low, high = cuts[part]
        return add(total, w_near[:, low:high], near[part])

    total = lax.optimization_barrier(dot(near_blocks[0, 0], charges))
    total = add(total, far_own, coeffs)
    total = add(total, w_mate, mate)
    total = add(total, w_far, jnp.concatenate(far))
    total = add_near(total, 0)
    low, high = cuts[-1]
    total = add(total, w_relay[:, :low], jnp.concatenate(relay[:-1]))
    total = add(total, w_relay[:, low:high], relay[-1])
    total = add_near(total, 1)
    total = add(total, far_other, jnp.where(is_inner, from_outer, from_inner))
    low, high = cuts[-1]
    return finish(total, three_pass(w_near[:, low:high]), near[-1])


def solution(mesh):
    in_specs = (
        P("leaf", "rhs"),
        P("leaf", None, None, None),
        P("leaf", None),
        P("leaf", None, None),
        P("leaf", None, None, None, None),
        P("leaf", None, None),
    )
    out_specs = P("leaf", "rhs")
    return jax.shard_map(
        per_device, mesh=mesh, in_specs=in_specs, out_specs=out_specs, check_vma=False
    )
```

```python
import jax
import jax.numpy as jnp
from jax import lax
from jax.experimental import pallas as pl
from jax.experimental.pallas import tpu as pltpu
from jax.sharding import PartitionSpec as P


HIGH = lax.Precision.HIGH


def dot(a, b):
    return jnp.dot(a, b, precision=HIGH)


def partner(value, distance, senders=None):
    everyone = range(lax.axis_size("leaf"))
    return lax.ppermute(value, "leaf", [(i, i ^ 1 << distance) for i in senders or everyone])


def two_along(sense, count):
    return [(i, (i + (2 if i % 2 else -2) * sense) % count) for i in range(count)]


def eighths(rows, *counts):
    edges = [rows * count // 64 * 8 for count in counts] + [rows]
    return list(zip([0] + edges, edges))


def three_pass(weight):
    high = lax.reduce_precision(weight, exponent_bits=8, mantissa_bits=7)
    parts = [high, weight - high, high]
    return jnp.concatenate([part.astype(jnp.bfloat16) for part in parts], axis=1)


def last_term(total_ref, left_ref, right_ref, out_ref, strips, sems):
    tile = strips.shape[2]
    copies = []
    for part in range(strips.shape[0]):
        columns = pl.ds(part * tile, tile)
        value = right_ref[:, columns]
        high = value.astype(jnp.bfloat16)
        low = (value - high.astype(jnp.float32)).astype(jnp.bfloat16)
        right = jnp.concatenate([high, high, low])
        term = jnp.dot(left_ref[...], right, preferred_element_type=jnp.float32)
        strips[part] = total_ref[:, columns] + term
        copy = pltpu.make_async_copy(strips.at[part], out_ref.at[:, columns], sems.at[part])
        copy.start()
        copies.append(copy)
    for copy in copies:
        copy.wait()


def finish(total, left, right):
    rows, cols = total.shape
    tile = min(cols, 256)
    local = pltpu.VMEM
    operands = [pltpu.with_memory_space_constraint(value, local) for value in (total, left, right)]
    depth = left.shape[1]
    return pl.pallas_call(
        last_term,
        out_shape=jax.ShapeDtypeStruct(total.shape, total.dtype),
        in_specs=[pl.BlockSpec(memory_space=local)] * len(operands),
        out_specs=pl.BlockSpec(memory_space=pl.ANY),
        scratch_shapes=[
            pltpu.VMEM((cols // tile, rows, tile), total.dtype),
            pltpu.SemaphoreType.DMA((cols // tile,)),
        ],
        cost_estimate=pl.CostEstimate(
            flops=2 * rows * cols * depth, bytes_accessed=8 * rows * cols, transcendentals=0
        ),
        compiler_params=pltpu.CompilerParams(vmem_limit_bytes=24 << 20),
    )(*operands)


def copy_rows(from_ref, to_ref, sem):
    copy = pltpu.make_async_copy(from_ref.at[pl.ds(0, to_ref.shape[0])], to_ref, sem)
    copy.start()
    copy.wait()


def first_rows(value, rows):
    shape = (rows, value.shape[1])
    return pl.pallas_call(
        copy_rows,
        out_shape=pltpu.VMEM(shape, value.dtype),
        in_specs=[pl.BlockSpec(memory_space=pl.ANY)],
        out_specs=pl.BlockSpec(memory_space=pltpu.VMEM),
        scratch_shapes=[pltpu.SemaphoreType.DMA(())],
        cost_estimate=pl.CostEstimate(
            flops=0, bytes_accessed=8 * rows * shape[1], transcendentals=0
        ),
        compiler_params=pltpu.CompilerParams(vmem_limit_bytes=8 << 20),
    )(value)


def per_device(charges, near_blocks, neighbours, compress, transfer, expand):
    count = lax.axis_size("leaf")
    here = lax.axis_index("leaf")
    side = jnp.where(here % 2 == 0, 1, -1)
    levels = count.bit_length() - 1
    last = levels - 1
    middle = count // 2
    outer = [i for i in range(count) if not middle // 2 <= i < count - middle // 2]
    inner = [i for i in range(count) if middle // 2 <= i < count - middle // 2]
    is_inner = (here >= middle // 2) & (here < count - middle // 2)
    shift = two_along(-1, count)
    central = [(s, t) for s, t in shift if abs(s - t) == 2 and (s < middle) != (t < middle)]
    others = [pair for pair in shift if pair not in central]
    over_middle = (here == middle) | (here == middle - 1)
    cuts = eighths(charges.shape[0], 4, 7)

    offsets = (neighbours[0] - here) % count
    offsets = jnp.where(offsets > count // 2, offsets - count, offsets)

    def weight(step):
        second = jnp.where(offsets[1] == step, near_blocks[0, 2], 0.0)
        return jnp.where(offsets[0] == step, near_blocks[0, 1], second)

    def move(value, pairs):
        return lax.ppermute(value, "leaf", pairs)

    def add(total, a, b):
        return lax.optimization_barrier(total + dot(a, b))

    far, near, relay = [], [], []
    leading_rows = first_rows(charges, cuts[0][1])
    coeffs = jnp.einsum("ar,ac->rc", compress[0], charges, precision=HIGH)
    later, coeffs = lax.optimization_barrier((charges, coeffs))
    for part, (low, high) in enumerate(cuts):
        rows = later[low:high] if part else leading_rows
        far.append(move(rows, two_along(1, count)))
        relay.append(partner(far[part], 0))
    near_central = move(leading_rows, central)
    near_others = move(leading_rows, others)
    near.append(jnp.where(over_middle, near_central, near_others))
    for part, (low, high) in enumerate(cuts[1:], 1):
        near.append(move(later[low:high], shift))
    mate = partner(charges, 0)
    for level in range(last):
        other = partner(coeffs, level)
        coeffs = dot(transfer[0, level, 0], coeffs) + dot(transfer[0, level, 1], other)
    from_outer = partner(coeffs, last, outer)
    from_inner = partner(coeffs, last, inner)
    ends = jnp.concatenate([transfer[0, last, 0], transfer[0, last, 1]], axis=1)
    far_own, far_other = jnp.split(dot(expand[0], ends), 2, axis=1)

    w_far, w_near, w_mate, w_relay = (weight(s) for s in (2 * side, -2 * side, side, -side))

    def add_near(total, part):
        low, high = cuts[part]
        return add(total, w_near[:, low:high], near[part])

    total = lax.optimization_barrier(dot(near_blocks[0, 0], charges))
    total = add(total, far_own, coeffs)
    total = add(total, w_mate, mate)
    total = add(total, w_far, jnp.concatenate(far))
    total = add_near(total, 0)
    low, high = cuts[-1]
    total = add(total, w_relay[:, :low], jnp.concatenate(relay[:-1]))
    total = add(total, w_relay[:, low:high], relay[-1])
    total = add_near(total, 1)
    total = add(total, far_other, jnp.where(is_inner, from_outer, from_inner))
    low, high = cuts[-1]
    return finish(total, three_pass(w_near[:, low:high]), near[-1])


def solution(mesh):
    in_specs = (
        P("leaf", "rhs"),
        P("leaf", None, None, None),
        P("leaf", None),
        P("leaf", None, None),
        P("leaf", None, None, None, None),
        P("leaf", None, None),
    )
    out_specs = P("leaf", "rhs")
    return jax.shard_map(
        per_device, mesh=mesh, in_specs=in_specs, out_specs=out_specs, check_vma=False
    )
```
